32 devices in a mesh: dp: 8 (over z, y), seq: 2 (over core), tensor: 2 (over x).
Axes of the slice: x: 2, y: 2, z: 4, core: 2. Of those that a mesh axis runs over, the one named last changes fastest.
Arguments:
- inputs: bfloat16 [8, 512, 1024], P('dp', 'seq'), may hold values from -6 to 6
- cotangent: bfloat16 [8, 512, 1024], P('dp', 'seq'), may hold values from -6 to 6
- segment_ids: int32 [8, 512], P('dp'), may hold values from 0 to 3, never falling along the last dimension, each value on 1 to 320 neighbouring positions
- mixer_params: float32 [2, 3030784], P('tensor', 'dp'), as said below
- mixer_moment: float32 [2, 3030784], P('tensor', 'dp'), may hold values from -4 to 4
- mixer_variance: float32 [2, 3030784], P('tensor', 'dp'), may hold values from 0.01 to 1
- dense_params: float32 [2, 3145728], P('tensor', 'dp'), as said below
- dense_moment: float32 [2, 3145728], P('tensor', 'dp'), may hold values from -4 to 4
- dense_variance: float32 [2, 3145728], P('tensor', 'dp'), may hold values from 0.01 to 1
- shared_params: float32 [263424], P('dp'), as said below
- shared_moment: float32 [263424], P('dp'), may hold values from -4 to 4
- shared_variance: float32 [263424], P('dp'), may hold values from 0.01 to 1
- scalar_params: float32 [2120], replicated, as said below
- scalar_moment: float32 [2120], replicated, may hold values from -4 to 4
- scalar_variance: float32 [2120], replicated, may hold values from 0.01 to 1
Outputs:
- block_output: bfloat16 [8, 512, 1024], P('dp', 'seq')
- input_gradient: float32 [8, 512, 1024], P('dp', 'seq')
- mixer_gradient: float32 [2, 3030784], P('tensor', 'dp')
- mixer_updated: float32 [2, 3030784], P('tensor', 'dp')
- moment_mixer: float32 [2, 3030784], P('tensor', 'dp')
- variance_mixer: float32 [2, 3030784], P('tensor', 'dp')
- dense_gradient: float32 [2, 3145728], P('tensor', 'dp')
- dense_updated: float32 [2, 3145728], P('tensor', 'dp')
- moment_dense: float32 [2, 3145728], P('tensor', 'dp')
- variance_dense: float32 [2, 3145728], P('tensor', 'dp')
- shared_gradient: float32 [263424], P('dp')
- shared_updated: float32 [263424], P('dp')
- moment_shared: float32 [263424], P('dp')
- variance_shared: float32 [263424], P('dp')
- scalar_gradient: float32 [2120], replicated
- scalar_updated: float32 [2120], replicated
- moment_scalar: float32 [2120], replicated
- variance_scalar: float32 [2120], replicated
The draws below stay inside these ranges and needn't reach their ends.
Inputs may be any that keep to these rules, and one draw needn't show every extreme that they name: `segment_ids`: segment numbers never fall along a sequence. `mixer_params`: matrices of order one over their fan-in, convolution taps and biases of order one half. `dense_params`: matrices of order one over their fan-in. `shared_params`: matrices of order one over their fan-in, convolution taps and biases of order one half. `scalar_params`: gains near one, a_log between 0 and log 16, softplus(dt_bias) between 0.001 and 0.1, d_skip between 0.5 and 1.5.
All inputs are finite; a program needn't handle non-finite values.
Results may differ from the reference program's by a relative error of at most 0.012.
The reference program's roundings to bfloat16 on the way count: a program that leaves them out, or rounds other values in their place, can miss the bound.
Values may be sent and summed in bfloat16 or wider, within the bound.
A program may use at most 192 MiB of HBM per device.

```python
import math
from functools import partial
import jax
import jax.numpy as jnp
import numpy as np
from jax import lax

D = 1024
HEADS = 24
HD = 64
NSTATE = 128
KCONV = 4
QH = 8
KVH = 2
AHD = 64
FF = 2048
SEQ_LEN = 512
STEP = 3
DSSM = 1536
HGROUPS = 2
HT = 12
CT = 768
QT = 4
KT = 1
FT = 1024
SEQS = 8
PM = 3030784
PF = 3145728
PS = 263424
PSM = 2120


def section_noise(key, full_shape, sections):
    noise_base = jax.random.normal(key, full_shape, jnp.float32)
    factor = jnp.concatenate([jnp.full((entry_count,), entry_scale, jnp.float32) for entry_count, entry_scale in sections])
    return noise_base * factor


def draw_mixer_params(key, part):
    sections = [(D * 2 * CT, D ** (-0.5)), (D * HT, 0.5 * D ** (-0.5)), (KCONV * CT, 0.5), (CT, 0.5), (CT * D, DSSM ** (-0.5)), (D * QT * AHD, D ** (-0.5)), (D * 2 * KT * AHD, D ** (-0.5)), (QT * AHD * D, AHD ** (-0.5))]
    return section_noise(key, (HGROUPS, PM), sections)


def draw_dense_params(key, part):
    sections = [(D * 2 * FT, D ** (-0.5)), (FT * D, FF ** (-0.5))]
    return section_noise(key, (HGROUPS, PF), sections)


def draw_shared_params(key, part):
    sections = [(D * 2 * NSTATE, D ** (-0.5)), (KCONV * 2 * NSTATE, 0.5), (2 * NSTATE, 0.5)]
    return section_noise(key, (PS,), sections)


def draw_scalar_params(key, part):
    subkeys = jax.random.split(key, 4)
    gains = 1.0 + 0.1 * jax.random.normal(subkeys[0], (2 * D,), jnp.float32)
    a_log = jax.random.uniform(subkeys[1], (HEADS,), jnp.float32, 0.0, math.log(16.0))
    step_init = jnp.exp(jax.random.uniform(subkeys[2], (HEADS,), jnp.float32, math.log(0.001), math.log(0.1)))
    dt_bias = step_init + jnp.log(-jnp.expm1(-step_init))
    d_skip = jax.random.uniform(subkeys[3], (HEADS,), jnp.float32, 0.5, 1.5)
    return jnp.concatenate([gains, a_log, dt_bias, d_skip])


def level_of(own_key, dims, cuts, smallest, largest):
    level = 1.0
    for axis_at, parts in cuts:
        draws = jax.random.uniform(jax.random.fold_in(jax.random.fold_in(own_key, 6), axis_at), (parts,), jnp.float32, smallest / len(cuts), largest / len(cuts))
        level = level * jnp.repeat(jnp.exp(draws), dims[axis_at] // parts).reshape((-1,) + (1,) * (len(dims) - 1 - axis_at))
    return level


def split_up(count, total, limit, lean):
    loads = [(1 << 20) // math.isqrt(standing ** lean) + 1 for standing in range(2, count + 1)]
    rest, counts = total - limit - (count - 1), [1] * (count - 1)
    while rest > 0:
        candidates = [i for i in range(count - 1) if counts[i] < limit]
        whole, left = sum([loads[i] for i in candidates]), rest
        for i in candidates:
            more = min(limit - counts[i], max(1, left * loads[i] // whole), rest)
            counts[i] = counts[i] + more
            rest = rest - more
    return np.array([limit] + counts)


def uneven(stream_key, number_of, total, limit, lean):
    if number_of == 2:
        one = jax.random.randint(stream_key, (), max(1, total - limit), min(limit, total - 1) + 1)
        return jnp.stack([one, total - one])
    sizes = jnp.asarray(split_up(number_of, total, limit, lean), jnp.int32)
    couples = (number_of - 1) // 2
    giver, sink = sizes[1:1 + 2 * couples:2], sizes[2:2 + 2 * couples:2]
    slack = jnp.minimum(giver - 1, limit - sink)
    passed = jax.random.randint(jax.random.fold_in(stream_key, 1), (couples,), 0, 1 << 20) % (slack + 1)
    sizes = sizes.at[1:1 + 2 * couples:2].set(giver - passed).at[2:2 + 2 * couples:2].set(sink + passed)
    return sizes[jax.random.permutation(jax.random.fold_in(stream_key, 2), number_of)]


def centred(own_key, dims, scale, bound, cuts=(), held_as=jnp.bfloat16):
    entries = scale * jax.random.normal(own_key, dims, jnp.float32)
    if cuts:
        entries = entries * level_of(own_key, dims, cuts, -0.22, 0.18)
    return jnp.clip(entries, -bound, bound).astype(held_as)


def setup_inputs(seed: int = 0) -> dict:
    arg_keys = jax.random.split(jax.random.key(seed), 16)
    inputs = centred(arg_keys[0], (SEQS, SEQ_LEN, D), 1.0, 6.0, ((0, 8), (1, 2)))
    cotangent = centred(arg_keys[1], (SEQS, SEQ_LEN, D), 1.0, 6.0, ((0, 8), (1, 2)))
    segment_ids = jax.vmap(lambda own: jnp.searchsorted(jnp.cumsum(uneven(own, 4, SEQ_LEN, SEQ_LEN * 5 // 8, 0)), jnp.arange(SEQ_LEN), side="right"))(jax.random.split(arg_keys[2], SEQS)).reshape((SEQS, SEQ_LEN)).astype(jnp.int32)
    mixer_params = draw_mixer_params(jax.random.fold_in(arg_keys[15], 71), 0)
    mixer_moment = centred(arg_keys[4], (HGROUPS, PM), 0.3, 4.0, ((0, 2), (1, 8)), jnp.float32)
    mixer_variance = jnp.clip(jnp.exp(math.log(1.0) - 4.6051702 * jax.random.uniform(arg_keys[5], (HGROUPS, PM), jnp.float32) ** level_of(arg_keys[5], (HGROUPS, PM), ((0, 2), (1, 8)), -0.2, 0.2)), 0.01, 1.0)
    dense_params = draw_dense_params(jax.random.fold_in(arg_keys[15], 71), 0)
    dense_moment = centred(arg_keys[7], (HGROUPS, PF), 0.3, 4.0, ((0, 2), (1, 8)), jnp.float32)
    dense_variance = jnp.clip(jnp.exp(math.log(1.0) - 4.6051702 * jax.random.uniform(arg_keys[8], (HGROUPS, PF), jnp.float32) ** level_of(arg_keys[8], (HGROUPS, PF), ((0, 2), (1, 8)), -0.2, 0.2)), 0.01, 1.0)
    shared_params = draw_shared_params(jax.random.fold_in(arg_keys[15], 71), 0)
    shared_moment = centred(arg_keys[10], (PS,), 0.3, 4.0, ((0, 8),), jnp.float32)
    shared_variance = jnp.clip(jnp.exp(math.log(1.0) - 4.6051702 * jax.random.uniform(arg_keys[11], (PS,), jnp.float32) ** level_of(arg_keys[11], (PS,), ((0, 8),), -0.2, 0.2)), 0.01, 1.0)
    scalar_params = draw_scalar_params(jax.random.fold_in(arg_keys[15], 71), 0)
    scalar_moment = centred(arg_keys[13], (PSM,), 0.3, 4.0, (), jnp.float32)
    scalar_variance = jnp.clip(jnp.exp(jax.random.uniform(arg_keys[14], (PSM,), jnp.float32, math.log(0.01), math.log(1.0))), 0.01, 1.0)
    return dict(inputs=inputs, cotangent=cotangent, segment_ids=segment_ids, mixer_params=mixer_params, mixer_moment=mixer_moment, mixer_variance=mixer_variance, dense_params=dense_params, dense_moment=dense_moment, dense_variance=dense_variance, shared_params=shared_params, shared_moment=shared_moment, shared_variance=shared_variance, scalar_params=scalar_params, scalar_moment=scalar_moment, scalar_variance=scalar_variance)


norm_eps = 1e-05
rope_base = 100000000000.0
highest = lax.Precision.HIGHEST
beta_first = 0.9
beta_second = 0.999
adam_eps = 1e-08
learn_rate = 0.01
decay_rate = 0.1
masked_score = -1e+30

def mixer_layout(model_width, channels, head_count, kernel, query_cols, key_cols):
    return [('w_zx', (model_width, 2, channels)), ('w_dt', (model_width, head_count)), ('conv_x', (kernel, channels)), ('conv_xb', (channels,)), ('w_out', (channels, model_width)), ('w_q', (model_width, query_cols)), ('w_kv', (model_width, 2, key_cols)), ('w_o', (query_cols, model_width))]

def dense_layout(model_width, hidden_units):
    return [('w_gu', (model_width, 2, hidden_units)), ('w_down', (hidden_units, model_width))]

def shared_layout(model_width, state_size, kernel):
    return [('w_bc', (model_width, 2 * state_size)), ('conv_bc', (kernel, 2 * state_size)), ('conv_bcb', (2 * state_size,))]

def scalar_layout(model_width, head_count):
    return [('gain_one', (model_width,)), ('gain_two', (model_width,)), ('a_log', (head_count,)), ('dt_bias', (head_count,)), ('d_skip', (head_count,))]

def unpack(flat_vector, layout):
    pieces = {}
    offset = 0
    for entry_name, entry_shape in layout:
        entry_size = math.prod(entry_shape)
        pieces[entry_name] = flat_vector[offset:offset + entry_size].reshape(entry_shape)
        offset = offset + entry_size
    return pieces

def pack(members):
    return jnp.concatenate([member.reshape(-1) for member in members])

def product(spec_text, left_side, right_side):
    return jnp.einsum(spec_text, left_side.astype(jnp.float32), right_side.astype(jnp.float32), precision=highest)

def rms_scale(values, gain):
    return values * lax.rsqrt(lax.optimization_barrier(jnp.mean(values * values, axis=-1, keepdims=True)) + norm_eps) * gain

def rope_angles(positions, head_dim):
    half_dim = head_dim // 2
    frequency = jnp.exp(jnp.arange(half_dim, dtype=jnp.float32) * (-2.0 * math.log(rope_base) / head_dim))
    return positions.astype(jnp.float32)[:, None] * frequency[None, :]

def rotate(vectors, angles):
    half_dim = vectors.shape[-1] // 2
    cosine = jnp.cos(angles)[:, None, :]
    sine = jnp.sin(angles)[:, None, :]
    first_half = vectors[..., :half_dim]
    second_half = vectors[..., half_dim:]
    return jnp.concatenate([first_half * cosine - second_half * sine, second_half * cosine + first_half * sine], axis=-1)

def causal_conv(extended, kernel_w, kernel_b, tap_mask):
    row_count = tap_mask.shape[1]
    summed = kernel_b
    for tap_index in range(kernel_w.shape[0]):
        summed = summed + tap_mask[:, :, tap_index, None] * kernel_w[tap_index] * extended[:, tap_index:tap_index + row_count]
    return summed

def mamba_front(ext_x, ext_bc, conv_x, conv_xb, conv_bc, conv_bcb, step_raw, dt_bias, a_log, tap_mask, head_dim, state_size):
    x_conv = jax.nn.silu(causal_conv(ext_x, conv_x, conv_xb, tap_mask))
    bc_conv = jax.nn.silu(causal_conv(ext_bc, conv_bc, conv_bcb, tap_mask))
    batch_size, row_count, channels = x_conv.shape
    x_heads = x_conv.reshape(batch_size, row_count, channels // head_dim, head_dim)
    step_size = jax.nn.softplus(step_raw + dt_bias)
    log_decay = -jnp.exp(a_log) * step_size
    return (x_heads, bc_conv[..., :state_size], bc_conv[..., state_size:], step_size, log_decay)

def ssd_output(x_heads, b_input, c_input, step_size, log_decay, d_skip, gate_z, state_in, seg_mask, carry_mask):
    cumulative = jnp.cumsum(log_decay, axis=1)
    log_gap = cumulative[:, :, None, :] - cumulative[:, None, :, :]
    decay_kernel = jnp.exp(jnp.where(seg_mask[..., None], log_gap, masked_score))
    inner_cb = jnp.einsum('btn,bsn->bts', c_input, b_input, precision=highest)
    weighted = x_heads * step_size[..., None]
    within = jnp.einsum('btsh,bshp->bthp', decay_kernel * inner_cb[..., None], weighted, precision=highest)
    carried = jnp.einsum('btn,bhpn->bthp', c_input, state_in, precision=highest) * (jnp.exp(cumulative) * carry_mask[..., None])[..., None]
    output = within + carried + d_skip[:, None] * x_heads
    batch_size, row_count = (output.shape[0], output.shape[1])
    return output.reshape(batch_size, row_count, -1) * jax.nn.silu(gate_z)

def attention_core(queries, keys_values, query_angles, key_angles, allowed):
    batch_size, query_rows, query_heads, head_dim = queries.shape
    key_heads = keys_values.shape[3]
    rotated_q = rotate(queries, query_angles).reshape(batch_size, query_rows, key_heads, query_heads // key_heads, head_dim)
    rotated_k = rotate(keys_values[:, :, 0], key_angles)
    values = keys_values[:, :, 1]
    scores = jnp.einsum('btgrd,bsgd->bgrts', rotated_q, rotated_k, precision=highest) * head_dim ** (-0.5)
    scores = jnp.where(allowed[:, None, None], scores, masked_score)
    row_peak = lax.stop_gradient(lax.optimization_barrier(jnp.max(scores, axis=-1, keepdims=True)))
    weights = jnp.exp(scores - row_peak)
    weights = weights / lax.optimization_barrier(jnp.sum(weights, axis=-1, keepdims=True))
    attended = jnp.einsum('bgrts,bsgd->btgrd', weights, values, precision=highest)
    return attended.reshape(batch_size, query_rows, query_heads * head_dim)

def adam_update(params, moment, variance, gradient, weight_decay):
    new_moment = beta_first * moment + (1.0 - beta_first) * gradient
    new_variance = beta_second * variance + (1.0 - beta_second) * gradient * gradient
    corrected = new_moment / (1.0 - beta_first ** STEP) / (jnp.sqrt(new_variance / (1.0 - beta_second ** STEP)) + adam_eps)
    return (params - learn_rate * (corrected + weight_decay * params), new_moment, new_variance)

def reference(inputs, cotangent, segment_ids, mixer_params, mixer_moment, mixer_variance, dense_params, dense_moment, dense_variance, shared_params, shared_moment, shared_variance, scalar_params, scalar_moment, scalar_variance):
    mixer_rows = [unpack(mixer_params[group_id].astype(jnp.bfloat16), mixer_layout(D, CT, HT, KCONV, QT * AHD, KT * AHD)) for group_id in range(HGROUPS)]
    dense_rows = [unpack(dense_params[group_id].astype(jnp.bfloat16), dense_layout(D, FT)) for group_id in range(HGROUPS)]
    shared = unpack(shared_params.astype(jnp.bfloat16), shared_layout(D, NSTATE, KCONV))
    scalars = unpack(scalar_params, scalar_layout(D, HEADS))
    full_zx = jnp.concatenate([group_w['w_zx'] for group_w in mixer_rows], axis=2)
    full_dt = jnp.concatenate([group_w['w_dt'] for group_w in mixer_rows], axis=1)
    full_cx = jnp.concatenate([group_w['conv_x'] for group_w in mixer_rows], axis=1).astype(jnp.float32)
    full_cxb = jnp.concatenate([group_w['conv_xb'] for group_w in mixer_rows], axis=0).astype(jnp.float32)
    full_out = jnp.concatenate([group_w['w_out'] for group_w in mixer_rows], axis=0)
    full_q = jnp.concatenate([group_w['w_q'] for group_w in mixer_rows], axis=1)
    full_kv = jnp.concatenate([group_w['w_kv'] for group_w in mixer_rows], axis=2)
    full_o = jnp.concatenate([group_w['w_o'] for group_w in mixer_rows], axis=0)
    full_gu = jnp.concatenate([group_w['w_gu'] for group_w in dense_rows], axis=2)
    full_down = jnp.concatenate([group_w['w_down'] for group_w in dense_rows], axis=0)
    conv_bc = shared['conv_bc'].astype(jnp.float32)
    conv_bcb = shared['conv_bcb'].astype(jnp.float32)
    positions = jnp.arange(SEQ_LEN)
    angles = rope_angles(positions, AHD)
    rim_rows = KCONV - 1

    def one_sequence(x_seq, cot_seq, seg_seq):
        x_float = x_seq[None].astype(jnp.float32)
        seg_row = seg_seq[None]
        norm_one_f, norm_one_vjp = jax.vjp(rms_scale, x_float, scalars['gain_one'])
        normed_one = norm_one_f.astype(jnp.bfloat16)
        mamba_input = product('btd,dcj->btcj', normed_one, full_zx).astype(jnp.bfloat16)
        state_input = product('btd,dj->btj', normed_one, shared['w_bc']).astype(jnp.bfloat16)
        step_input = product('btd,dh->bth', normed_one, full_dt)
        query_input = product('btd,dj->btj', normed_one, full_q).astype(jnp.bfloat16)
        keyval_input = product('btd,dcj->btcj', normed_one, full_kv).astype(jnp.bfloat16)
        ext_seg = jnp.concatenate([jnp.full((1, rim_rows), -1, jnp.int32), seg_row.astype(jnp.int32)], axis=1)
        tap_mask = jnp.stack([(ext_seg[:, tap_index:tap_index + SEQ_LEN] == seg_row).astype(jnp.float32) for tap_index in range(KCONV)], axis=-1)
        lower = positions[:, None] >= positions[None, :]
        seg_mask = (seg_row[:, :, None] == seg_row[:, None, :]) & lower[None]
        carry_zero = jnp.zeros((1, SEQ_LEN), jnp.float32)
        state_zero = jnp.zeros((1, HT, HD, NSTATE), jnp.float32)
        ext_bc = jnp.concatenate([jnp.zeros((1, rim_rows, 2 * NSTATE), jnp.float32), state_input.astype(jnp.float32)], axis=1)
        group_vjps = []
        gated_parts = []
        for group_id in range(HGROUPS):
            chan_slice = slice(group_id * CT, (group_id + 1) * CT)
            head_slice = slice(group_id * HT, (group_id + 1) * HT)
            ext_x = jnp.concatenate([jnp.zeros((1, rim_rows, CT), jnp.float32), mamba_input[:, :, 1, chan_slice].astype(jnp.float32)], axis=1)
            gate_z = mamba_input[:, :, 0, chan_slice].astype(jnp.float32)

            def group_fn(ext_xin, ext_bcin, conv_xw, conv_xbw, conv_bcw, conv_bcbw, step_raw, dt_bias, a_log, d_skip, gate_in):
                front_out = mamba_front(ext_xin, ext_bcin, conv_xw, conv_xbw, conv_bcw, conv_bcbw, step_raw, dt_bias, a_log, tap_mask=tap_mask, head_dim=HD, state_size=NSTATE)
                return ssd_output(front_out[0], front_out[1], front_out[2], front_out[3], front_out[4], d_skip, gate_in, state_zero, seg_mask=seg_mask, carry_mask=carry_zero)
            gated_part, group_vjp = jax.vjp(group_fn, ext_x, ext_bc, full_cx[:, chan_slice], full_cxb[chan_slice], conv_bc, conv_bcb, step_input[:, :, head_slice], scalars['dt_bias'][head_slice], scalars['a_log'][head_slice], scalars['d_skip'][head_slice], gate_z)
            gated_parts.append(gated_part)
            group_vjps.append(group_vjp)
        gated_bf = jnp.concatenate(gated_parts, axis=2).astype(jnp.bfloat16)
        query_f = query_input.astype(jnp.float32).reshape(1, SEQ_LEN, QH, AHD)
        keyval_f = keyval_input.astype(jnp.float32).reshape(1, SEQ_LEN, 2, KVH, AHD)
        attend = partial(attention_core, query_angles=angles, key_angles=angles, allowed=seg_mask)
        attended, attend_vjp = jax.vjp(attend, query_f, keyval_f)
        attended_bf = attended.astype(jnp.bfloat16)
        residual = x_float + product('btj,jd->btd', attended_bf, full_o) + product('btj,jd->btd', gated_bf, full_out)
        norm_two_f, norm_two_vjp = jax.vjp(rms_scale, residual, scalars['gain_two'])
        normed_two = norm_two_f.astype(jnp.bfloat16)
        gate_up = product('btd,dcf->btcf', normed_two, full_gu)
        gate_part = gate_up[:, :, 0]
        up_part = gate_up[:, :, 1]
        activated = (jax.nn.silu(gate_part) * up_part).astype(jnp.bfloat16)
        block_out = (residual + product('btf,fd->btd', activated, full_down)).astype(jnp.bfloat16)
        cot_bf = cot_seq[None]
        grad_act = product('btd,fd->btf', cot_bf, full_down)
        grad_wdown = product('btf,btd->fd', activated, cot_bf)
        sigmoid_gate = jax.nn.sigmoid(gate_part)
        grad_gate = grad_act * up_part * sigmoid_gate * (1.0 + gate_part * (1.0 - sigmoid_gate))
        grad_up = grad_act * gate_part * sigmoid_gate
        grad_gu = jnp.stack([grad_gate, grad_up], axis=2).astype(jnp.bfloat16)
        grad_wgu = product('btd,btcf->dcf', normed_two, grad_gu)
        grad_norm_two = product('btcf,dcf->btd', grad_gu, full_gu)
        grad_res_norm, grad_gain_two = norm_two_vjp(grad_norm_two)
        grad_residual = cot_bf.astype(jnp.float32) + grad_res_norm
        grad_mix = grad_residual.astype(jnp.bfloat16)
        grad_wo = product('btj,btd->jd', attended_bf, grad_mix)
        grad_wout = product('btj,btd->jd', gated_bf, grad_mix)
        grad_attended = product('btd,jd->btj', grad_mix, full_o)
        grad_gated = product('btd,jd->btj', grad_mix, full_out)
        grad_query, grad_keyval = attend_vjp(grad_attended)
        grad_z_parts = []
        grad_x_parts = []
        grad_step_parts = []
        grad_cx_parts = []
        grad_cxb_parts = []
        grad_dtb_parts = []
        grad_alog_parts = []
        grad_skip_parts = []
        grad_cbc = jnp.zeros((KCONV, 2 * NSTATE), jnp.float32)
        grad_cbcb = jnp.zeros((2 * NSTATE,), jnp.float32)
        grad_wbc = jnp.zeros((D, 2 * NSTATE), jnp.float32)
        grad_norm_bc = jnp.zeros((1, SEQ_LEN, D), jnp.float32)
        for group_id in range(HGROUPS):
            chan_slice = slice(group_id * CT, (group_id + 1) * CT)
            group_grads = group_vjps[group_id](grad_gated[:, :, chan_slice])
            grad_x_parts.append(group_grads[0][:, rim_rows:])
            grad_bc_bf = group_grads[1][:, rim_rows:].astype(jnp.bfloat16)
            grad_wbc = grad_wbc + product('btd,btj->dj', normed_one, grad_bc_bf)
            grad_norm_bc = grad_norm_bc + product('btj,dj->btd', grad_bc_bf, shared['w_bc'])
            grad_cx_parts.append(group_grads[2])
            grad_cxb_parts.append(group_grads[3])
            grad_cbc = grad_cbc + group_grads[4]
            grad_cbcb = grad_cbcb + group_grads[5]
            grad_step_parts.append(group_grads[6])
            grad_dtb_parts.append(group_grads[7])
            grad_alog_parts.append(group_grads[8])
            grad_skip_parts.append(group_grads[9])
            grad_z_parts.append(group_grads[10])
        grad_zx_bf = jnp.stack([jnp.concatenate(grad_z_parts, axis=2), jnp.concatenate(grad_x_parts, axis=2)], axis=2).astype(jnp.bfloat16)
        grad_step_bf = jnp.concatenate(grad_step_parts, axis=2).astype(jnp.bfloat16)
        grad_q_bf = grad_query.reshape(1, SEQ_LEN, QH * AHD).astype(jnp.bfloat16)
        grad_kv_bf = grad_keyval.reshape(1, SEQ_LEN, 2, KVH * AHD).astype(jnp.bfloat16)
        grad_wzx = product('btd,btcj->dcj', normed_one, grad_zx_bf)
        grad_wdt = product('btd,bth->dh', normed_one, grad_step_bf)
        grad_wq = product('btd,btj->dj', normed_one, grad_q_bf)
        grad_wkv = product('btd,btcj->dcj', normed_one, grad_kv_bf)
        grad_norm_one = product('btcj,dcj->btd', grad_zx_bf, full_zx) + product('bth,dh->btd', grad_step_bf, full_dt) + product('btj,dj->btd', grad_q_bf, full_q) + product('btcj,dcj->btd', grad_kv_bf, full_kv) + grad_norm_bc
        grad_x_norm, grad_gain_one = norm_one_vjp(grad_norm_one)
        input_grad = grad_residual + grad_x_norm
        gradients = (grad_wzx, grad_wdt, jnp.concatenate(grad_cx_parts, axis=1), jnp.concatenate(grad_cxb_parts, axis=0), grad_wout, grad_wq, grad_wkv, grad_wo, grad_wgu, grad_wdown, grad_wbc, grad_cbc, grad_cbcb, grad_gain_one, grad_gain_two, jnp.concatenate(grad_alog_parts), jnp.concatenate(grad_dtb_parts), jnp.concatenate(grad_skip_parts))
        return (block_out[0], input_grad[0], gradients)

    def sequence_step(carry, packed_seq):
        out_seq, grad_seq, gradients = one_sequence(packed_seq[0], packed_seq[1], packed_seq[2])
        return (tuple((carry_term + new_term for carry_term, new_term in zip(carry, gradients))), (out_seq, grad_seq))
    grad_shapes = [(D, 2, DSSM), (D, HEADS), (KCONV, DSSM), (DSSM,), (DSSM, D), (D, QH * AHD), (D, 2, KVH * AHD), (QH * AHD, D), (D, 2, FF), (FF, D), (D, 2 * NSTATE), (KCONV, 2 * NSTATE), (2 * NSTATE,), (D,), (D,), (HEADS,), (HEADS,), (HEADS,)]
    initial = tuple((jnp.zeros(grad_shape, jnp.float32) for grad_shape in grad_shapes))
    totals, outputs = lax.scan(sequence_step, initial, (inputs, cotangent, segment_ids))
    block_output, input_gradient = outputs
    mixer_rows_g = []
    dense_rows_g = []
    for group_id in range(HGROUPS):
        chan_slice = slice(group_id * CT, (group_id + 1) * CT)
        head_slice = slice(group_id * HT, (group_id + 1) * HT)
        query_slice = slice(group_id * QT * AHD, (group_id + 1) * QT * AHD)
        key_slice = slice(group_id * KT * AHD, (group_id + 1) * KT * AHD)
        hidden_slice = slice(group_id * FT, (group_id + 1) * FT)
        mixer_rows_g.append(pack([totals[0][:, :, chan_slice], totals[1][:, head_slice], totals[2][:, chan_slice], totals[3][chan_slice], totals[4][chan_slice], totals[5][:, query_slice], totals[6][:, :, key_slice], totals[7][query_slice]]))
        dense_rows_g.append(pack([totals[8][:, :, hidden_slice], totals[9][hidden_slice]]))
    mixer_gradient = jnp.stack(mixer_rows_g)
    dense_gradient = jnp.stack(dense_rows_g)
    shared_gradient = pack([totals[10], totals[11], totals[12]])
    scalar_gradient = pack([totals[13], totals[14], totals[15], totals[16], totals[17]])
    mixer_new = adam_update(mixer_params, mixer_moment, mixer_variance, mixer_gradient, decay_rate)
    dense_new = adam_update(dense_params, dense_moment, dense_variance, dense_gradient, decay_rate)
    shared_new = adam_update(shared_params, shared_moment, shared_variance, shared_gradient, decay_rate)
    scalar_new = adam_update(scalar_params, scalar_moment, scalar_variance, scalar_gradient, 0.0)
    return (block_output, input_gradient, mixer_gradient, mixer_new[0], mixer_new[1], mixer_new[2], dense_gradient, dense_new[0], dense_new[1], dense_new[2], shared_gradient, shared_new[0], shared_new[1], shared_new[2], scalar_gradient, scalar_new[0], scalar_new[1], scalar_new[2])
```

```python
from functools import partial
import math

import jax
import jax.numpy as jnp
from jax import lax
from jax.experimental import pallas as pl
from jax.experimental.pallas import tpu as pltpu
from jax.sharding import PartitionSpec as P

HEADS = 24
HD = 64
NSTATE = 128
KCONV = 4
QH = 8
KVH = 2
AHD = 64
FF = 2048
STEP = 3


norm_eps = 1e-05
rope_base = 100000000000.0
highest = lax.Precision.HIGHEST
beta_first = 0.9
beta_second = 0.999
adam_eps = 1e-08
learn_rate = 0.01
decay_rate = 0.1
masked_score = -1e30


def from_behind(x, axis, by):
    size = lax.axis_size(axis)
    pairs = [(i, i + by) for i in range(size) if 0 <= i + by < size]
    return lax.ppermute(x, axis, pairs)


def prefix(x, axis, combine, identity):
    size, index = (lax.axis_size(axis), lax.axis_index(axis))
    everything = jax.tree.map(lambda part: lax.all_gather(part, axis), x)
    start = jax.tree.map(
        lambda part, zero: jnp.broadcast_to(jnp.asarray(zero, part.dtype), part.shape), x, identity
    )

    def hop(k, before):
        reached = k < index
        new = combine(before, jax.tree.map(lambda part: part[k], everything))
        return jax.tree.map(lambda a, b: jnp.where(reached, a, b), new, before)

    return lax.fori_loop(0, size, hop, start)


def prefix_2(x, axis, combine, identity):
    size, index = (lax.axis_size(axis), lax.axis_index(axis))
    everything = jax.tree.map(
        lambda part, kind: lax.all_gather(part.astype(kind), axis),
        x,
        jax.tree.map(lambda a: jnp.bfloat16 if a.dtype == jnp.float32 else a.dtype, x),
    )
    start = jax.tree.map(
        lambda part, zero: jnp.broadcast_to(jnp.asarray(zero, part.dtype), part.shape), x, identity
    )

    def hop(k, before):
        at = size - 1 - k
        reached = at > index
        new = combine(
            before, jax.tree.map(lambda part, own: part[at].astype(own.dtype), everything, x)
        )
        return jax.tree.map(lambda a, b: jnp.where(reached, a, b), new, before)

    return lax.fori_loop(0, size, hop, start)


LANES = 128
TILE = 4096
ANY = pl.BlockSpec(memory_space=pl.ANY)
barrier = lax.optimization_barrier


def swap(x, axis):
    return lax.ppermute(x, axis, [(0, 1), (1, 0)])


def pair_sum(x, axis):
    if lax.axis_size(axis) != 2:
        return lax.psum(x, axis)
    own = barrier(x.astype(jnp.bfloat16))
    return own.astype(jnp.float32) + barrier(swap(own, axis)).astype(jnp.float32)


def gather_kernel(n, nb, *refs):
    ins, outs = refs[:nb], refs[nb : 2 * nb]
    up_s, up_r, dn_s, dn_r, y_s, y_r, c_s, c_r, l_s = refs[2 * nb :]
    me, core, group = lax.axis_index("dp"), lax.axis_index("seq"), lax.axis_index("tensor")
    line = n // 2
    m, y = lax.div(me, 2), lax.rem(me, 2)
    halves = [r.shape[0] // 2 for r in ins]

    def dst(b, s, c):
        return outs[b].at[s, pl.ds(c * halves[b], halves[b])]

    def link(b, s, c, src, send, recv, to_dp, to_core):
        return pltpu.make_async_remote_copy(
            src_ref=src,
            dst_ref=dst(b, s, c),
            send_sem=send.at[b, s],
            recv_sem=recv.at[b, s],
            device_id=(to_dp, to_core, group),
            device_id_type=pl.DeviceIdType.MESH,
        )

    def up(b, s, src=None):
        return link(b, s, core, dst(b, s, core) if src is None else src, up_s, up_r, me + 2, core)

    def down(b, s, src=None):
        return link(b, s, core, dst(b, s, core) if src is None else src, dn_s, dn_r, me - 2, core)

    def side(b, s, src=None):
        to = me + 1 - 2 * y
        return link(b, s, core, dst(b, s, core) if src is None else src, y_s, y_r, to, core)

    def across(b, s, c):
        return link(b, s, c, dst(b, s, c), c_s, c_r, me, 1 - core)

    own = [ins[b].at[pl.ds(core * halves[b], halves[b])] for b in range(nb)]
    local = [pltpu.make_async_copy(ins[b], outs[b].at[me], l_s.at[b]) for b in range(nb)]
    can_up, can_down = m + 1 < line, m > 0
    for b in range(nb):

        @pl.when(can_up)
        def _():
            up(b, me, own[b]).start()

        @pl.when(can_down)
        def _():
            down(b, me, own[b]).start()

        side(b, me, own[b]).start()
        local[b].start()
    other = me + 1 - 2 * y

    def from_side(b, s):
        side(b, s).wait_recv()
        across(b, s, core).start()

    def each(d, fn_below, fn_above):
        @pl.when(m - d >= 0)
        def _():
            for b in range(nb):
                fn_below(b)

        @pl.when(m + d < line)
        def _():
            for b in range(nb):
                fn_above(b)

    for d in range(1, line + 1):
        if d < line:

            def below(b):
                s = me - 2 * d
                up(b, s).wait_recv()

                @pl.when(can_up)
                def _():
                    up(b, s).start()

                side(b, s).start()
                across(b, s, core).start()

            def above(b):
                s = me + 2 * d
                down(b, s).wait_recv()

                @pl.when(can_down)
                def _():
                    down(b, s).start()

                side(b, s).start()
                across(b, s, core).start()

            each(d, below, above)
        e = d - 1
        if e == 0:
            for b in range(nb):
                from_side(b, other)
        else:
            each(e, lambda b: from_side(b, other - 2 * e), lambda b: from_side(b, other + 2 * e))
    for b in range(nb):
        local[b].wait()

        @pl.when(can_up)
        def _():
            up(b, me, own[b]).wait_send()

        @pl.when(can_down)
        def _():
            down(b, me, own[b]).wait_send()

        side(b, me, own[b]).wait_send()
        across(b, other, core).wait_send()
        across(b, other, 1 - core).wait_recv()
    for d in range(1, line):

        def below_end(b):
            s = me - 2 * d

            @pl.when(can_up)
            def _():
                up(b, s).wait_send()

            side(b, s).wait_send()
            for t in (s, other - 2 * d):
                across(b, t, core).wait_send()
                across(b, t, 1 - core).wait_recv()

        def above_end(b):
            s = me + 2 * d

            @pl.when(can_down)
            def _():
                down(b, s).wait_send()

            side(b, s).wait_send()
            for t in (s, other + 2 * d):
                across(b, t, core).wait_send()
                across(b, t, 1 - core).wait_recv()

        each(d, below_end, above_end)


def gather_all(shards):
    n, nb = lax.axis_size("dp"), len(shards)
    sem = pltpu.SemaphoreType.DMA((nb, n))
    return pl.pallas_call(
        partial(gather_kernel, n, nb),
        out_shape=[jax.ShapeDtypeStruct((n,) + s.shape, s.dtype) for s in shards],
        in_specs=[ANY] * nb,
        out_specs=[ANY] * nb,
        scratch_shapes=[sem] * 8 + [pltpu.SemaphoreType.DMA((nb,))],
        compiler_params=pltpu.CompilerParams(has_side_effects=True),
        name="weights_gather",
    )(*shards)


def exchange_kernel(n, nb, *refs):
    ins, outs = refs[: nb + 1], refs[nb + 1 : 2 * nb + 2]
    send, recv, l_s = refs[2 * nb + 2 :]
    me, core, group = lax.axis_index("dp"), lax.axis_index("seq"), lax.axis_index("tensor")

    def link(b, d):
        to = lax.rem(me + d, n)
        return pltpu.make_async_remote_copy(
            src_ref=ins[b].at[to] if b < nb else ins[b],
            dst_ref=outs[b].at[me],
            send_sem=send.at[b, d],
            recv_sem=recv.at[b, d],
            device_id=(to, core, group),
            device_id_type=pl.DeviceIdType.MESH,
        )

    def arrival(b, d):
        source = lax.rem(me - d + n, n)
        return pltpu.make_async_remote_copy(
            src_ref=outs[b].at[source],
            dst_ref=outs[b].at[source],
            send_sem=send.at[b, d],
            recv_sem=recv.at[b, d],
            device_id=(source, core, group),
            device_id_type=pl.DeviceIdType.MESH,
        )

    local = [
        pltpu.make_async_copy(ins[b].at[me] if b < nb else ins[b], outs[b].at[me], l_s.at[b])
        for b in range(nb + 1)
    ]
    for d in range(n - 1, 0, -1):
        for b in range(nb + 1):
            link(b, d).start()
    for b in range(nb + 1):
        local[b].start()
    for b in range(nb + 1):
        local[b].wait()
    for d in range(1, n):
        for b in range(nb + 1):
            arrival(b, d).wait_recv()
            link(b, d).wait_send()


def exchange_all(pieces, everywhere):
    n, nb = lax.axis_size("dp"), len(pieces)
    shapes = [jax.ShapeDtypeStruct(p.shape, p.dtype) for p in pieces]
    shapes.append(jax.ShapeDtypeStruct((n,) + everywhere.shape, everywhere.dtype))
    return pl.pallas_call(
        partial(exchange_kernel, n, nb),
        out_shape=shapes,
        in_specs=[ANY] * (nb + 1),
        out_specs=[ANY] * (nb + 1),
        scratch_shapes=[
            pltpu.SemaphoreType.DMA((nb + 1, n)),
            pltpu.SemaphoreType.DMA((nb + 1, n)),
            pltpu.SemaphoreType.DMA((nb + 1,)),
        ],
        compiler_params=pltpu.CompilerParams(has_side_effects=True),
        name="gradients_exchange",
    )(*pieces, everywhere)


def aligned_shard(flat):
    n, index, size = lax.axis_size("dp"), lax.axis_index("dp"), flat.shape[0]
    firsts = [-(-k * size // TILE) for k in range(n + 1)]
    rows = max(firsts[k + 1] - firsts[k] for k in range(n)) * (TILE // LANES)
    flat = barrier(flat)
    if size % TILE:
        part = from_behind(flat[:TILE].astype(jnp.bfloat16), "dp", -1).astype(jnp.float32)
        flat = jnp.concatenate([flat, part, jnp.zeros((TILE,), jnp.float32)])
        lead = lax.rem(TILE - lax.rem(index * size, TILE), TILE)
        flat = barrier(lax.dynamic_slice_in_dim(flat, lead, rows * LANES))
    return flat.reshape(rows, LANES).astype(jnp.bfloat16)


def full_rows(gathered, size):
    n = gathered.shape[0]
    if size % TILE == 0:
        return gathered.reshape(-1, LANES)
    firsts = [-(-k * size // TILE) for k in range(n + 1)]
    per = TILE // LANES
    return jnp.concatenate(
        [gathered[k, : (firsts[k + 1] - firsts[k]) * per] for k in range(n)], axis=0
    )


def unpack_rows(rows, layout):
    rows = barrier(rows.astype(jnp.float32))
    pieces, offset = {}, 0
    for entry_name, entry_shape in layout:
        entry_rows = math.prod(entry_shape) // LANES
        piece = rows[offset : offset + entry_rows]
        pieces[entry_name] = barrier(piece.reshape(entry_shape)).astype(jnp.bfloat16)
        offset = offset + entry_rows
    return pieces


def owner_pieces(members, size):
    n = lax.axis_size("dp")
    starts = [k * size // TILE for k in range(n)]
    count = max(-(-(k + 1) * size // TILE) - starts[k] for k in range(n))
    per = TILE // LANES
    rows = [barrier(member.reshape(-1, LANES)) for member in members]
    short = (starts[-1] + count) * per - n * size // LANES
    if short:
        rows.append(jnp.zeros((short, LANES), jnp.float32))
    if len(rows) > 3:
        rows[1:4] = [jnp.concatenate(rows[1:4], axis=0)]
        height, offset, placed = sum(r.shape[0] for r in rows), 0, 0.0
        for r in rows:
            after = height - offset - r.shape[0]
            placed = placed + lax.pad(r, jnp.float32(0), ((offset, after, 0), (0, 0, 0)))
            offset = offset + r.shape[0]
        rows = barrier(placed)
    else:
        rows = barrier(jnp.concatenate(rows, axis=0))
    if size % TILE == 0:
        return rows.reshape(n, count * per, LANES).astype(jnp.bfloat16)
    cut = [rows[first * per : (first + count) * per].astype(jnp.bfloat16) for first in starts]
    return jnp.stack(cut)


def own_shard(rows, size):
    flat = rows.reshape(-1)
    if size % TILE == 0:
        return flat
    return lax.dynamic_slice_in_dim(flat, lax.rem(lax.axis_index("dp") * size, TILE), size)


def hops(parts_to, axis="dp"):
    n = lax.axis_size(axis)
    return [
        lax.ppermute(parts_to(d), axis, [(i, (i + d) % n) for i in range(n)]) for d in range(1, n)
    ]


def gather_beside(shard):
    n, me, core = lax.axis_size("dp"), lax.axis_index("dp"), lax.axis_index("seq")
    half = shard.shape[0] // 2
    mine = lax.dynamic_slice_in_dim(shard, core * half, half)
    came = [mine] + hops(lambda d: mine)
    block = barrier(jnp.stack(came[::-1] * 2))
    block = lax.dynamic_slice_in_dim(block, n - 1 - me, n)
    partner = swap(barrier(block), "seq")
    low = jnp.where(core == 0, block, partner)
    high = jnp.where(core == 0, partner, block)
    return jnp.concatenate([low, high], axis=1)


def core_halves(piece):
    core = lax.axis_index("seq")
    half = piece.shape[1] // 2
    away = lax.dynamic_slice_in_dim(piece, (1 - core) * half, half, axis=1)
    mine = lax.dynamic_slice_in_dim(piece, core * half, half, axis=1)
    arrived = swap(away, "seq")
    return (mine.astype(jnp.float32) + arrived.astype(jnp.float32)).astype(jnp.bfloat16)


def rejoin(total, size):
    core = lax.axis_index("seq")
    partner = swap(total, "seq")
    low = jnp.where(core == 0, total, partner)
    high = jnp.where(core == 0, partner, total)
    return own_shard(jnp.concatenate([low, high], axis=0), size)


def reduce_beside(piece, size):
    n, me = lax.axis_size("dp"), lax.axis_index("dp")
    summed = barrier(core_halves(piece))

    def part(d):
        return lax.dynamic_index_in_dim(summed, lax.rem(me + d, n), 0, keepdims=False)

    total = part(0).astype(jnp.float32)
    for came in hops(part):
        total = total + came.astype(jnp.float32)
    return rejoin(total, size)


def reduce_to_owners(pieces, sizes, everywhere):
    scalars = everywhere + swap(everywhere, "seq")
    *received, scalars = exchange_all([core_halves(piece) for piece in pieces], scalars)
    owned = [
        rejoin(jnp.sum(part.astype(jnp.float32), axis=0), size)
        for part, size in zip(received, sizes)
    ]
    return owned, jnp.sum(scalars, axis=0)


def mixer_layout(model_width, channels, head_count, kernel, query_cols, key_cols):
    return [
        ("w_zx", (model_width, 2 * channels)),
        ("w_dt", (model_width, head_count)),
        ("conv_x", (kernel, channels)),
        ("conv_xb", (channels,)),
        ("w_out", (channels, model_width)),
        ("w_q", (model_width, query_cols)),
        ("w_kv", (model_width, 2 * key_cols)),
        ("w_o", (query_cols, model_width)),
    ]


def dense_layout(model_width, hidden_units):
    return [("w_gu", (model_width, 2 * hidden_units)), ("w_down", (hidden_units, model_width))]


def shared_layout(model_width, state_size, kernel):
    return [
        ("w_bc", (model_width, 2 * state_size)),
        ("conv_bc", (kernel, 2 * state_size)),
        ("conv_bcb", (2 * state_size,)),
    ]


def scalar_layout(model_width, head_count):
    return [
        ("gain_one", (model_width,)),
        ("gain_two", (model_width,)),
        ("a_log", (head_count,)),
        ("dt_bias", (head_count,)),
        ("d_skip", (head_count,)),
    ]


def unpack(flat_vector, layout):
    pieces = {}
    offset = 0
    for entry_name, entry_shape in layout:
        entry_size = math.prod(entry_shape)
        pieces[entry_name] = flat_vector[offset : offset + entry_size].reshape(entry_shape)
        offset = offset + entry_size
    return pieces


def pack(members):
    return jnp.concatenate([member.reshape(-1) for member in members])


def matmul(spec_text, left_side, right_side):
    return jnp.einsum(spec_text, left_side, right_side, preferred_element_type=jnp.float32)


def rms_scale(values, gain):
    return values * lax.rsqrt(jnp.mean(values * values, axis=-1, keepdims=True) + norm_eps) * gain


def rope_angles(positions, head_dim):
    half_dim = head_dim // 2
    frequency = jnp.exp(
        jnp.arange(half_dim, dtype=jnp.float32) * (-2.0 * math.log(rope_base) / head_dim)
    )
    return positions.astype(jnp.float32)[:, None] * frequency[None, :]


def rotate(vectors, angles):
    half_dim = vectors.shape[-1] // 2
    cosine = jnp.cos(angles)[:, None, :]
    sine = jnp.sin(angles)[:, None, :]
    first_half = vectors[..., :half_dim]
    second_half = vectors[..., half_dim:]
    return jnp.concatenate(
        [first_half * cosine - second_half * sine, second_half * cosine + first_half * sine],
        axis=-1,
    )


def causal_conv(extended, kernel_w, kernel_b, tap_mask):
    row_count = tap_mask.shape[1]
    summed = kernel_b
    for tap_index in range(kernel_w.shape[0]):
        summed = (
            summed
            + tap_mask[:, :, tap_index, None]
            * kernel_w[tap_index]
            * extended[:, tap_index : tap_index + row_count]
        )
    return summed


def mamba_front(
    ext_x,
    ext_bc,
    conv_x,
    conv_xb,
    conv_bc,
    conv_bcb,
    step_raw,
    dt_bias,
    a_log,
    tap_mask,
    head_dim,
    state_size,
):
    x_conv = jax.nn.silu(causal_conv(ext_x, conv_x, conv_xb, tap_mask))
    bc_conv = jax.nn.silu(causal_conv(ext_bc, conv_bc, conv_bcb, tap_mask))
    batch_size, row_count, channels = x_conv.shape
    x_heads = x_conv.reshape(batch_size, row_count, channels // head_dim, head_dim)
    step_size = jax.nn.softplus(step_raw + dt_bias)
    log_decay = -jnp.exp(a_log) * step_size
    return (x_heads, bc_conv[..., :state_size], bc_conv[..., state_size:], step_size, log_decay)


def ssd_output(
    x_heads, b_input, c_input, step_size, log_decay, d_skip, gate_z, state_in, seg_mask, carry_mask
):
    cumulative = jnp.cumsum(log_decay, axis=1)
    log_gap = cumulative[:, :, None, :] - cumulative[:, None, :, :]
    decay_kernel = jnp.exp(jnp.where(seg_mask[..., None], log_gap, masked_score))
    inner_cb = jnp.einsum("btn,bsn->bts", c_input, b_input, precision=highest)
    weighted = x_heads * step_size[..., None]
    within = jnp.einsum(
        "btsh,bshp->bthp", decay_kernel * inner_cb[..., None], weighted, precision=highest
    )
    carried = (
        jnp.einsum("btn,bhpn->bthp", c_input, state_in, precision=highest)
        * (jnp.exp(cumulative) * carry_mask[..., None])[..., None]
    )
    output = within + carried + d_skip[:, None] * x_heads
    batch_size, row_count = (output.shape[0], output.shape[1])
    return output.reshape(batch_size, row_count, -1) * jax.nn.silu(gate_z)


def block_decay(log_decay, dec_flag):
    return jnp.exp(jnp.sum(log_decay, axis=1)) * dec_flag[:, None]


def state_final(x_heads, b_input, step_size, log_decay, state_in, last_mask, dec_flag):
    cumulative = jnp.cumsum(log_decay, axis=1)
    final_log = cumulative[:, -1]
    weight_row = jnp.exp(final_log[:, None, :] - cumulative) * last_mask[..., None] * step_size
    gathered = jnp.einsum(
        "bshp,bsn->bhpn", weight_row[..., None] * x_heads, b_input, precision=highest
    )
    return block_decay(log_decay, dec_flag)[..., None, None] * state_in + gathered


def combine_states(earlier, later):
    return (earlier[0] * later[0], later[1] + later[0][..., None, None] * earlier[1])


def attention_core(queries, keys_values, query_angles, key_angles, allowed):
    batch_size, query_rows, query_heads, head_dim = queries.shape
    key_heads = keys_values.shape[3]
    rotated_q = rotate(queries, query_angles).reshape(
        batch_size, query_rows, key_heads, query_heads // key_heads, head_dim
    )
    rotated_k = rotate(keys_values[:, :, 0], key_angles)
    values = keys_values[:, :, 1]
    scores = jnp.einsum(
        "btgrd,bsgd->bgrts", rotated_q, rotated_k, precision=highest
    ) * head_dim ** (-0.5)
    scores = jnp.where(allowed[:, None, None], scores, masked_score)
    row_peak = lax.stop_gradient(jnp.max(scores, axis=-1, keepdims=True))
    weights = jnp.exp(scores - row_peak)
    weights = weights / jnp.sum(weights, axis=-1, keepdims=True)
    attended = jnp.einsum("bgrts,bsgd->btgrd", weights, values, precision=highest)
    return attended.reshape(batch_size, query_rows, query_heads * head_dim)


def adam_update(params, moment, variance, gradient, weight_decay):
    new_moment = beta_first * moment + (1.0 - beta_first) * gradient
    new_variance = beta_second * variance + (1.0 - beta_second) * gradient * gradient
    corrected = (
        new_moment
        / (1.0 - beta_first**STEP)
        / (jnp.sqrt(new_variance / (1.0 - beta_second**STEP)) + adam_eps)
    )
    return (params - learn_rate * (corrected + weight_decay * params), new_moment, new_variance)


def body(
    inputs,
    cotangent,
    segment_ids,
    mixer_params,
    mixer_moment,
    mixer_variance,
    dense_params,
    dense_moment,
    dense_variance,
    shared_params,
    shared_moment,
    shared_variance,
    scalar_params,
    scalar_moment,
    scalar_variance,
):
    group_count = lax.axis_size("tensor")
    group_index = lax.axis_index("tensor")
    block_index = lax.axis_index("seq")
    mamba_heads = HEADS // group_count
    mamba_channels = mamba_heads * HD
    query_heads = QH // group_count
    key_heads = KVH // group_count
    hidden_units = FF // group_count
    rim_rows = KCONV - 1
    batch_size, row_count, model_width = inputs.shape
    sizes = (mixer_params.shape[1], dense_params.shape[1], shared_params.shape[0])
    shards = [aligned_shard(flat) for flat in (mixer_params[0], dense_params[0], shared_params)]
    beside = lax.axis_size("dp") <= 8
    if beside:
        mixer_all, shared_all = gather_all([shards[0], shards[2]])
        held = barrier(shards[1] + barrier(mixer_all[0, 0, :1] * 0))
        dense_all = gather_beside(held)
    else:
        mixer_all, dense_all, shared_all = gather_all(shards)
    mixer_w = unpack_rows(
        full_rows(mixer_all, sizes[0]),
        mixer_layout(
            model_width, mamba_channels, mamba_heads, KCONV, query_heads * AHD, key_heads * AHD
        ),
    )
    shared = unpack_rows(
        full_rows(shared_all, sizes[2]), shared_layout(model_width, NSTATE, KCONV)
    )
    scalars = unpack(scalar_params, scalar_layout(model_width, HEADS))
    head_start = group_index * mamba_heads
    alog_local = lax.dynamic_slice_in_dim(scalars["a_log"], head_start, mamba_heads)
    dtb_local = lax.dynamic_slice_in_dim(scalars["dt_bias"], head_start, mamba_heads)
    skip_local = lax.dynamic_slice_in_dim(scalars["d_skip"], head_start, mamba_heads)
    row_start = block_index * row_count
    rows_iota = jnp.arange(row_count)
    local_seg = lax.dynamic_slice_in_dim(segment_ids, row_start, row_count, axis=1)
    prior_seg = lax.dynamic_slice_in_dim(
        segment_ids, jnp.maximum(block_index - 1, 0) * row_count, row_count, axis=1
    )
    has_prior = block_index > 0
    ext_seg = jnp.concatenate([prior_seg[:, row_count - rim_rows :], local_seg], axis=1)
    ext_valid = jnp.concatenate(
        [jnp.broadcast_to(has_prior, (rim_rows,)), jnp.ones((row_count,), jnp.bool_)]
    )
    tap_mask = jnp.stack(
        [
            (
                ext_valid[tap_index : tap_index + row_count]
                & (ext_seg[:, tap_index : tap_index + row_count] == local_seg)
            ).astype(jnp.float32)
            for tap_index in range(KCONV)
        ],
        axis=-1,
    )
    seg_mask = (local_seg[:, :, None] == local_seg[:, None, :]) & (
        rows_iota[:, None] >= rows_iota[None, :]
    )[None]
    continues = has_prior & (local_seg[:, 0] == prior_seg[:, -1])
    carry_mask = (continues[:, None] & (local_seg == local_seg[:, :1])).astype(jnp.float32)
    last_mask = (local_seg == local_seg[:, -1:]).astype(jnp.float32)
    dec_flag = (continues & (local_seg[:, -1] == local_seg[:, 0])).astype(jnp.float32)
    query_pos = row_start + rows_iota
    key_pos = jnp.concatenate([query_pos - row_count, query_pos])
    key_seg = jnp.concatenate([prior_seg, local_seg], axis=1)
    key_valid = jnp.concatenate(
        [jnp.broadcast_to(has_prior, (row_count,)), jnp.ones((row_count,), jnp.bool_)]
    )
    allowed = (
        key_valid[None, None, :]
        & (key_pos[None, None, :] <= query_pos[None, :, None])
        & (key_seg[:, None, :] == local_seg[:, :, None])
    )
    x_float = inputs.astype(jnp.float32)
    norm_one_f, norm_one_vjp = jax.vjp(rms_scale, x_float, scalars["gain_one"])
    normed_one = norm_one_f.astype(jnp.bfloat16)
    mamba_input = matmul("btd,dj->btj", normed_one, mixer_w["w_zx"]).astype(jnp.bfloat16)
    gate_raw, x_raw = mamba_input[..., :mamba_channels], mamba_input[..., mamba_channels:]
    state_input = matmul("btd,dj->btj", normed_one, shared["w_bc"]).astype(jnp.bfloat16)
    step_input = matmul("btd,dh->bth", normed_one, mixer_w["w_dt"])
    query_input = matmul("btd,dj->btj", normed_one, mixer_w["w_q"]).astype(jnp.bfloat16)
    keyval_input = (
        matmul("btd,dj->btj", normed_one, mixer_w["w_kv"])
        .astype(jnp.bfloat16)
        .reshape(batch_size, row_count, -1)
    )
    tail_rows = jnp.concatenate(
        [x_raw[:, row_count - rim_rows :], state_input[:, row_count - rim_rows :]], axis=-1
    )
    prior_keyval, prior_tail = from_behind((keyval_input, tail_rows), "seq", 1)
    ext_x = jnp.concatenate(
        [prior_tail[..., :mamba_channels], x_raw], axis=1
    ).astype(jnp.float32)
    ext_bc = jnp.concatenate([prior_tail[..., mamba_channels:], state_input], axis=1).astype(
        jnp.float32
    )
    front = partial(mamba_front, tap_mask=tap_mask, head_dim=HD, state_size=NSTATE)
    front_out, front_vjp = jax.vjp(
        front,
        ext_x,
        ext_bc,
        mixer_w["conv_x"].astype(jnp.float32),
        mixer_w["conv_xb"].astype(jnp.float32),
        shared["conv_bc"].astype(jnp.float32),
        shared["conv_bcb"].astype(jnp.float32),
        step_input,
        dtb_local,
        alog_local,
    )
    x_heads, b_input, c_input, step_size, log_decay = front_out
    gate_z = gate_raw.astype(jnp.float32)
    final_fn = partial(state_final, last_mask=last_mask, dec_flag=dec_flag)
    block_dec = block_decay(log_decay, dec_flag)
    local_state = final_fn(
        x_heads,
        b_input,
        step_size,
        log_decay,
        jnp.zeros((batch_size, mamba_heads, HD, NSTATE), jnp.float32),
    )
    scan_identity = (jnp.ones_like(block_dec), jnp.zeros_like(local_state))
    if lax.axis_size("seq") == 2:
        state_in = from_behind(local_state, "seq", 1)
    else:
        state_in = prefix((block_dec, local_state), "seq", combine_states, scan_identity)[1]
    ssd_fn = partial(ssd_output, seg_mask=seg_mask, carry_mask=carry_mask)
    gated_out, ssd_vjp = jax.vjp(
        ssd_fn, x_heads, b_input, c_input, step_size, log_decay, skip_local, gate_z, state_in
    )
    gated_bf = gated_out.astype(jnp.bfloat16)
    query_f = query_input.astype(jnp.float32).reshape(batch_size, row_count, query_heads, AHD)
    keyval_all = (
        jnp.concatenate([prior_keyval, keyval_input], axis=1)
        .astype(jnp.float32)
        .reshape(batch_size, 2 * row_count, 2, key_heads, AHD)
    )
    attend = partial(
        attention_core,
        query_angles=rope_angles(query_pos, AHD),
        key_angles=rope_angles(key_pos, AHD),
        allowed=allowed,
    )
    attended, attend_vjp = jax.vjp(attend, query_f, keyval_all)
    attended_bf = attended.astype(jnp.bfloat16)
    mixer_part = matmul("btj,jd->btd", attended_bf, mixer_w["w_o"]) + matmul(
        "btj,jd->btd", gated_bf, mixer_w["w_out"]
    )
    residual = x_float + pair_sum(mixer_part, "tensor")
    norm_two_f, norm_two_vjp = jax.vjp(rms_scale, residual, scalars["gain_two"])
    normed_two = norm_two_f.astype(jnp.bfloat16)
    dense_w = unpack_rows(full_rows(dense_all, sizes[1]), dense_layout(model_width, hidden_units))
    gate_up = matmul("btd,df->btf", normed_two, dense_w["w_gu"])
    gate_part = gate_up[..., :hidden_units]
    up_part = gate_up[..., hidden_units:]
    activated = (jax.nn.silu(gate_part) * up_part).astype(jnp.bfloat16)
    dense_part = matmul("btf,fd->btd", activated, dense_w["w_down"])
    block_output = (residual + pair_sum(dense_part, "tensor")).astype(jnp.bfloat16)
    grad_act = matmul("btd,fd->btf", cotangent, dense_w["w_down"])
    grad_wdown = matmul("btf,btd->fd", activated, cotangent)
    sigmoid_gate = jax.nn.sigmoid(gate_part)
    grad_gate = grad_act * up_part * sigmoid_gate * (1.0 + gate_part * (1.0 - sigmoid_gate))
    grad_up = grad_act * gate_part * sigmoid_gate
    grad_gu = jnp.concatenate([grad_gate, grad_up], axis=2).astype(jnp.bfloat16)
    grad_wgu = matmul("btd,btf->df", normed_two, grad_gu)
    dense_pieces = owner_pieces([grad_wgu, grad_wdown], sizes[1])
    if beside:
        dense_owned = reduce_beside(dense_pieces, sizes[1])
    grad_norm_two = pair_sum(matmul("btf,df->btd", grad_gu, dense_w["w_gu"]), "tensor")
    grad_res_norm, grad_gain_two = norm_two_vjp(grad_norm_two)
    grad_residual = cotangent.astype(jnp.float32) + grad_res_norm
    grad_mix = grad_residual.astype(jnp.bfloat16)
    grad_wo = matmul("btj,btd->jd", attended_bf, grad_mix)
    grad_wout = matmul("btj,btd->jd", gated_bf, grad_mix)
    grad_attended = matmul("btd,jd->btj", grad_mix, mixer_w["w_o"])
    grad_gated = matmul("btd,jd->btj", grad_mix, mixer_w["w_out"])
    grad_query, grad_keyval = attend_vjp(grad_attended)
    grad_xh, grad_b, grad_c, grad_step, grad_log, grad_skip, grad_z, grad_state = ssd_vjp(
        grad_gated
    )
    if lax.axis_size("seq") == 2:
        state_back = from_behind(barrier(grad_state.astype(jnp.bfloat16)), "seq", -1)
        state_back = state_back.astype(jnp.float32)
    else:
        state_back = prefix_2((block_dec, grad_state), "seq", combine_states, scan_identity)[1]
    final_vjp = jax.vjp(final_fn, x_heads, b_input, step_size, log_decay, state_in)[1]
    extra_xh, extra_b, extra_step, extra_log, extra_state = final_vjp(state_back)
    front_grads = front_vjp(
        (grad_xh + extra_xh, grad_b + extra_b, grad_c, grad_step + extra_step, grad_log + extra_log)
    )
    (
        grad_ext_x,
        grad_ext_bc,
        grad_cx,
        grad_cxb,
        grad_cbc,
        grad_cbcb,
        grad_step_in,
        grad_dtb,
        grad_alog,
    ) = front_grads
    tail_grad = jnp.concatenate([grad_ext_x[:, :rim_rows], grad_ext_bc[:, :rim_rows]], axis=-1)
    prior_grad = grad_keyval[:, :row_count].reshape(batch_size, row_count, -1)
    next_keyval, next_tail = (
        from_behind(prior_grad.astype(jnp.bfloat16), "seq", -1).astype(prior_grad.dtype),
        from_behind(tail_grad.astype(jnp.bfloat16), "seq", -1).astype(tail_grad.dtype),
    )
    grad_x_raw = (
        grad_ext_x[:, rim_rows:].at[:, row_count - rim_rows :].add(next_tail[..., :mamba_channels])
    )
    grad_bc_raw = (
        grad_ext_bc[:, rim_rows:].at[:, row_count - rim_rows :].add(next_tail[..., mamba_channels:])
    )
    grad_kv_bf = (
        (grad_keyval[:, row_count:].reshape(batch_size, row_count, -1) + next_keyval)
        .astype(jnp.bfloat16)
    )
    grad_zx_bf = jnp.concatenate([grad_z, grad_x_raw], axis=2).astype(jnp.bfloat16)
    grad_q_bf = grad_query.reshape(batch_size, row_count, -1).astype(jnp.bfloat16)
    grad_step_bf = grad_step_in.astype(jnp.bfloat16)
    grad_bc_bf = grad_bc_raw.astype(jnp.bfloat16)
    grad_wzx = matmul("btd,btj->dj", normed_one, grad_zx_bf)
    grad_wdt = matmul("btd,bth->dh", normed_one, grad_step_bf)
    grad_wq = matmul("btd,btj->dj", normed_one, grad_q_bf)
    grad_wkv = matmul("btd,btj->dj", normed_one, grad_kv_bf)
    grad_wbc_part = matmul("btd,btj->dj", normed_one, grad_bc_bf)
    grad_norm_part = (
        matmul("btj,dj->btd", grad_zx_bf, mixer_w["w_zx"])
        + matmul("bth,dh->btd", grad_step_bf, mixer_w["w_dt"])
        + matmul("btj,dj->btd", grad_q_bf, mixer_w["w_q"])
        + matmul("btj,dj->btd", grad_kv_bf, mixer_w["w_kv"])
        + matmul("btj,dj->btd", grad_bc_bf, shared["w_bc"])
    )
    head_grads = lax.dynamic_update_slice_in_dim(
        jnp.zeros((3, HEADS), jnp.float32),
        jnp.stack([grad_alog, grad_dtb, grad_skip]),
        head_start,
        axis=1,
    )
    grad_norm_one = pair_sum(grad_norm_part, "tensor")
    if group_count == 2:
        head_all = head_grads + swap(head_grads, "tensor")
    else:
        head_all = lax.psum(head_grads, "tensor")
    grad_x_norm, grad_gain_one = norm_one_vjp(grad_norm_one)
    input_gradient = grad_residual + grad_x_norm
    mixer_pieces = owner_pieces(
        [grad_wzx, grad_wdt, grad_cx, grad_cxb, grad_wout, grad_wq, grad_wkv, grad_wo], sizes[0]
    )
    shared_pieces = owner_pieces([grad_wbc_part, grad_cbc, grad_cbcb], sizes[2])
    scalar_local = pack([grad_gain_one, grad_gain_two, head_all])
    scalar_size = scalar_local.shape[0]
    scalar_rows = jnp.pad(scalar_local, (0, -scalar_size % (8 * LANES))).reshape(-1, LANES)
    pieces, piece_sizes = [mixer_pieces, shared_pieces], [sizes[0], sizes[2]]
    if not beside:
        pieces, piece_sizes = pieces + [dense_pieces], piece_sizes + [sizes[1]]
    owned, scalar_rows = reduce_to_owners(pieces, piece_sizes, scalar_rows)
    mixer_owned, shared_owned = owned[:2]
    if not beside:
        dense_owned = owned[2]
    mixer_gradient, dense_gradient = mixer_owned[None], dense_owned[None]
    shared_gradient = pair_sum(shared_owned, "tensor")
    scalar_gradient = scalar_rows.reshape(-1)[:scalar_size]
    mixer_new = adam_update(mixer_params, mixer_moment, mixer_variance, mixer_gradient, decay_rate)
    dense_new = adam_update(dense_params, dense_moment, dense_variance, dense_gradient, decay_rate)
    shared_new = adam_update(
        shared_params, shared_moment, shared_variance, shared_gradient, decay_rate
    )
    scalar_new = adam_update(scalar_params, scalar_moment, scalar_variance, scalar_gradient, 0.0)
    return (
        block_output,
        input_gradient,
        mixer_gradient,
        mixer_new[0],
        mixer_new[1],
        mixer_new[2],
        dense_gradient,
        dense_new[0],
        dense_new[1],
        dense_new[2],
        shared_gradient,
        shared_new[0],
        shared_new[1],
        shared_new[2],
        scalar_gradient,
        scalar_new[0],
        scalar_new[1],
        scalar_new[2],
    )


def solution(mesh):
    return jax.shard_map(
        body,
        mesh=mesh,
        in_specs=(
            P("dp", "seq", None),
            P("dp", "seq", None),
            P("dp", None),
            P("tensor", "dp"),
            P("tensor", "dp"),
            P("tensor", "dp"),
            P("tensor", "dp"),
            P("tensor", "dp"),
            P("tensor", "dp"),
            P("dp"),
            P("dp"),
            P("dp"),
            P(),
            P(),
            P(),
        ),
        out_specs=(
            P("dp", "seq", None),
            P("dp", "seq", None),
            P("tensor", "dp"),
            P("tensor", "dp"),
            P("tensor", "dp"),
            P("tensor", "dp"),
            P("tensor", "dp"),
            P("tensor", "dp"),
            P("tensor", "dp"),
            P("tensor", "dp"),
            P("dp"),
            P("dp"),
            P("dp"),
            P("dp"),
            P(),
            P(),
            P(),
            P(),
        ),
        check_vma=False,
    )
```
